32 devices in a mesh: inst: 2 (over y), space: 16 (over z, x, core).
Axes of the slice: x: 2, y: 2, z: 4, core: 2. Of those that a mesh axis runs over, the one named last changes fastest.
Arguments:
- flow_state: float32 [4, 4, 192, 8, 512], P('inst', None, 'space'), may hold values from -6 to 6
- radial_first: float32 [512, 512], replicated, may hold values from -0.25 to 0.25
- radial_second: float32 [512, 512], replicated, may hold values from -0.25 to 0.25
- radial_flow: float32 [192, 512], P('space'), may hold values from -6 to 6
- swirl_flow: float32 [512, 192], replicated, may hold values from -6 to 6
- radius_inverse: float32 [512], replicated, may hold values from 0.05 to 1
- radial_flux: float32 [4, 4], replicated, may hold values from -3 to 3
- swirl_flux: float32 [4, 4], replicated, may hold values from -3 to 3
- cross_flux: float32 [4, 4], replicated, may hold values from -3 to 3
- span_flux: float32 [4, 4], replicated, may hold values from -3 to 3
- frequency: float32 [1], replicated, may hold values from 0.5 to 1.5
- viscosity: float32 [1], replicated, may hold values from 0.05 to 0.3
Outputs:
- residual: float32 [4, 4, 192, 8, 512], P('inst', None, 'space')
The draws below stay inside these ranges and needn't reach their ends.
All inputs are finite; a program needn't handle non-finite values.
Results may differ from the reference program's by a relative error of at most 0.000055.
Values sent between devices are 32-bit elements; how exact they have to be, the bound alone decides.
A program may use at most 64 MiB of HBM per device.

```python
import math
import jax
import jax.numpy as jnp
from jax import lax

RADIAL = 512
AZIMUTH = 192
VARS = 4
PLANES = 8
INSTANCES = 4


def block_levels(rng, dims, shards, least, top_value):
    level, own = 1.0, jax.random.fold_in(rng, 6)
    for axis_at, parts in shards:
        steps = jnp.exp(jax.random.uniform(jax.random.fold_in(own, axis_at), (parts,), jnp.float32, least / len(shards), top_value / len(shards)))
        level = level * jnp.repeat(steps, dims[axis_at] // parts).reshape([-1 if axis == axis_at else 1 for axis in range(len(dims))])
    return level


def gaussian(own_key, extent, scale, bound, pieces=(), dtype=jnp.bfloat16):
    level = block_levels(own_key, extent, pieces, -0.22, 0.18) if pieces else 1.0
    drawn = jax.random.normal(own_key, extent, jnp.float32) * scale * level
    return jnp.minimum(jnp.maximum(drawn, -bound), bound).astype(dtype)


def setup_inputs(seed: int = 0) -> dict:
    key_of = jax.random.split(jax.random.key(seed), 13)
    return {
        "flow_state": gaussian(key_of[0], (INSTANCES, VARS, AZIMUTH, PLANES, RADIAL), 1.0, 6.0, ((0, 2), (2, 16)), jnp.float32),
        "radial_first": gaussian(key_of[1], (RADIAL, RADIAL), RADIAL ** -0.5, 0.25, (), jnp.float32),
        "radial_second": gaussian(key_of[2], (RADIAL, RADIAL), RADIAL ** -0.5, 0.25, (), jnp.float32),
        "radial_flow": gaussian(key_of[3], (AZIMUTH, RADIAL), 1.0, 6.0, ((0, 16),), jnp.float32),
        "swirl_flow": gaussian(key_of[4], (RADIAL, AZIMUTH), 1.0, 6.0, (), jnp.float32),
        "radius_inverse": jnp.clip(jnp.exp(jax.random.uniform(key_of[5], (RADIAL,), jnp.float32, math.log(0.05), math.log(1.0))), 0.05, 1.0),
        "radial_flux": gaussian(key_of[6], (VARS, VARS), VARS ** -0.5, 3.0, (), jnp.float32),
        "swirl_flux": gaussian(key_of[7], (VARS, VARS), VARS ** -0.5, 3.0, (), jnp.float32),
        "cross_flux": gaussian(key_of[8], (VARS, VARS), VARS ** -0.5, 3.0, (), jnp.float32),
        "span_flux": gaussian(key_of[9], (VARS, VARS), VARS ** -0.5, 3.0, (), jnp.float32),
        "frequency": jnp.clip(jax.random.uniform(key_of[10], (1,), jnp.float32, 0.5, 1.5), 0.5, 1.5),
        "viscosity": jnp.clip(jax.random.uniform(key_of[11], (1,), jnp.float32, 0.05, 0.3), 0.05, 0.3),
    }


highest = lax.Precision.HIGHEST


def spectral(points):
    indices = jnp.arange(points)
    offsets = (indices[:, None] - indices[None, :]) % points
    spacing = 2.0 * math.pi / points
    angles = offsets.astype(jnp.float32) * (math.pi / points)
    parity = (1 - 2 * (offsets % 2)).astype(jnp.float32)
    nonzero = offsets != 0
    sines = jnp.where(nonzero, jnp.sin(angles), jnp.float32(1.0))
    first = jnp.where(nonzero, 0.5 * parity * jnp.cos(angles) / sines, jnp.float32(0.0))
    diagonal_value = -math.pi ** 2 / (3.0 * spacing ** 2) - 1.0 / 6.0
    second = jnp.where(nonzero, -0.5 * parity / (sines * sines), jnp.float32(diagonal_value))
    return first, second


def apply_flux(matrix, fields):
    return jnp.einsum('uv,v...->u...', matrix, fields, precision=highest)


def reference(flow_state, radial_first, radial_second, radial_flow, swirl_flow, radius_inverse, radial_flux, swirl_flux, cross_flux, span_flux, frequency, viscosity):
    time_matrix, unused = spectral(INSTANCES)
    turn_first, turn_second = spectral(AZIMUTH)
    spacing = 2.0 * math.pi / AZIMUTH
    turn_first = spacing * turn_first
    turn_second = (spacing * spacing) * turn_second
    coupled = frequency[0] * jnp.einsum('nm,mvtzr->nvtzr', time_matrix, flow_state, precision=highest)
    swirl_coeff = (swirl_flow.T * radius_inverse[None, :])[:, None, :]
    radial_coeff = radial_flow[:, None, :]
    viscous = viscosity[0]

    def one_instance(fields):
        radial_slope = jnp.einsum('vtzs,rs->vtzr', fields, radial_first, precision=highest)
        radial_curve = jnp.einsum('vtzs,rs->vtzr', fields, radial_second, precision=highest)
        turn_slope = jnp.einsum('st,vtzr->vszr', turn_first, fields, precision=highest)
        turn_curve = jnp.einsum('st,vtzr->vszr', turn_second, fields, precision=highest)
        cross_slope = jnp.einsum('st,vtzr->vszr', turn_first, radial_slope, precision=highest)
        upper = jnp.roll(fields, -1, axis=2)
        lower = jnp.roll(fields, 1, axis=2)
        span_slope = 0.5 * (upper - lower)
        span_curve = upper + lower - 2.0 * fields
        turning = swirl_coeff * turn_slope + radius_inverse * apply_flux(swirl_flux, turn_slope)
        turning = turning + radius_inverse * apply_flux(cross_flux, cross_slope)
        turning = turning - viscous * (radius_inverse * radius_inverse) * turn_curve
        radial_part = radial_coeff * radial_slope + apply_flux(radial_flux, radial_slope)
        radial_part = radial_part - viscous * (radial_curve + radius_inverse * radial_slope)
        radial_part = radial_part + apply_flux(span_flux, span_slope) - viscous * span_curve
        return turning + radial_part

    return coupled + lax.map(one_instance, flow_state)
```

```python
import math

import jax
import jax.numpy as jnp
from jax import lax
from jax.sharding import PartitionSpec as P

highest = lax.Precision.HIGHEST


def spectral(points):
    indices = jnp.arange(points)
    offsets = (indices[:, None] - indices[None, :]) % points
    spacing = 2.0 * math.pi / points
    angles = offsets.astype(jnp.float32) * (math.pi / points)
    parity = (1 - 2 * (offsets % 2)).astype(jnp.float32)
    nonzero = offsets != 0
    sines = jnp.where(nonzero, jnp.sin(angles), jnp.float32(1.0))
    first = jnp.where(nonzero, 0.5 * parity * jnp.cos(angles) / sines, jnp.float32(0.0))
    diagonal_value = -math.pi**2 / (3.0 * spacing**2) - 1.0 / 6.0
    second = jnp.where(nonzero, -0.5 * parity / (sines * sines), jnp.float32(diagonal_value))
    return (first, second)


def apply_flux(matrix, fields):
    return jnp.einsum("uv,iv...->iu...", matrix, fields, precision=highest)


def on_device_lines(
    flow_state,
    radial_first,
    radial_second,
    radial_flow,
    swirl_flow,
    radius_inverse,
    radial_flux,
    swirl_flux,
    cross_flux,
    span_flux,
    frequency,
    viscosity,
):
    inst_dev = flow_state.shape[0]
    n_inst = lax.axis_size("inst")
    n_space = lax.axis_size("space")
    instances = inst_dev * n_inst
    time_matrix, unused = spectral(instances)
    azimuth = swirl_flow.shape[1]
    radial = flow_state.shape[4]
    planes = flow_state.shape[3]
    turn_first, turn_second = spectral(azimuth)
    spacing = 2.0 * math.pi / azimuth
    turn_first = spacing * turn_first
    turn_second = spacing * spacing * turn_second
    viscous = viscosity[0]
    radial_slope = jnp.einsum("ivtzs,rs->ivtzr", flow_state, radial_first, precision=highest)
    radial_curve = jnp.einsum("ivtzs,rs->ivtzr", flow_state, radial_second, precision=highest)
    lane = math.gcd(radial, planes * radial // n_space)
    row_total = planes * radial // lane
    shape_rows = flow_state.shape[:3] + (row_total, lane)
    state_rows = flow_state.reshape(shape_rows)
    slope_rows = radial_slope.reshape(shape_rows)
    fields = lax.all_to_all(state_rows, "space", split_axis=3, concat_axis=2, tiled=True)
    slopes = lax.all_to_all(slope_rows, "space", split_axis=3, concat_axis=2, tiled=True)
    row_offset = lax.axis_index("space") * fields.shape[3]
    turning_fields = fields
    turning_slopes = slopes
    item_count = turning_fields.shape[0]
    variables = turning_fields.shape[1]
    count = turning_fields.shape[3]
    lane = turning_fields.shape[4]
    width = count * lane
    row_ids = row_offset + jnp.arange(count, dtype=jnp.int32)
    blocks = row_ids % (radial // lane)
    point_ids = (blocks[:, None] * lane + jnp.arange(lane, dtype=jnp.int32)[None, :]).reshape(width)
    inverse_tile = jnp.take(radius_inverse, point_ids)
    swirl_tile = jnp.take(swirl_flow, point_ids, axis=0).T * inverse_tile[None, :]
    turning_fields = turning_fields.reshape(item_count, variables, azimuth, width)
    turning_slopes = turning_slopes.reshape(item_count, variables, azimuth, width)
    turn_slope = jnp.einsum("st,ivtc->ivsc", turn_first, turning_fields, precision=highest)
    turn_curve = jnp.einsum("st,ivtc->ivsc", turn_second, turning_fields, precision=highest)
    cross_slope = jnp.einsum("st,ivtc->ivsc", turn_first, turning_slopes, precision=highest)
    turned_term = swirl_tile * turn_slope + inverse_tile * apply_flux(swirl_flux, turn_slope)
    turned_term = turned_term + inverse_tile * apply_flux(cross_flux, cross_slope)
    turned_term = turned_term - viscous * (inverse_tile * inverse_tile) * turn_curve
    result = lax.all_to_all(
        turned_term.reshape(item_count, variables, azimuth, count, lane),
        "space",
        split_axis=2,
        concat_axis=3,
        tiled=True,
    )
    turned = result.reshape(flow_state.shape)
    own_rows = lax.dynamic_slice_in_dim(time_matrix, lax.axis_index("inst") * inst_dev, inst_dev, 0)
    mixed_out = jnp.einsum(
        "nm,mvtzr->nvtzr",
        own_rows,
        lax.all_gather(flow_state, "inst", axis=0, tiled=True),
        precision=highest,
    )
    far_terms = frequency[0] * mixed_out + turned
    upper = jnp.roll(flow_state, -1, axis=3)
    lower = jnp.roll(flow_state, 1, axis=3)
    span_slope = 0.5 * (upper - lower)
    span_curve = upper + lower - 2.0 * flow_state
    radial_part = radial_flow[:, None, :] * radial_slope + apply_flux(radial_flux, radial_slope)
    radial_part = radial_part - viscous * (radial_curve + radius_inverse * radial_slope)
    radial_part = radial_part + apply_flux(span_flux, span_slope) - viscous * span_curve
    return far_terms + radial_part


def mix(matrix, fields):
    return jnp.stack(
        [
            sum(matrix[u, v] * fields[:, v] for v in range(fields.shape[1]))
            for u in range(matrix.shape[0])
        ],
        axis=1,
    )


def product(spec, *operands):
    return jnp.einsum(spec, *operands, precision=lax.Precision.HIGH)


def on_device(
    flow_state,
    radial_first,
    radial_second,
    radial_flow,
    swirl_flow,
    radius_inverse,
    radial_flux,
    swirl_flux,
    cross_flux,
    span_flux,
    frequency,
    viscosity,
):
    inst_dev, variables, azimuth_dev, planes, radial = flow_state.shape
    n_inst = lax.axis_size("inst")
    n_space = lax.axis_size("space")
    azimuth = swirl_flow.shape[1]
    viscous = viscosity[0]
    time_matrix, unused = spectral(inst_dev * n_inst)
    turn_first, turn_second = spectral(azimuth)
    spacing = 2.0 * math.pi / azimuth
    turn_first = spacing * turn_first
    turn_second = spacing * spacing * turn_second
    inst_at = lax.axis_index("inst")
    own_rows = lax.dynamic_slice_in_dim(time_matrix, inst_at * inst_dev, inst_dev, 0)
    weights = frequency[0] * own_rows
    coupled = 0.0
    for shift in range(n_inst):
        ring = [((at + shift) % n_inst, at) for at in range(n_inst)]
        state = lax.ppermute(flow_state, "inst", ring) if shift else flow_state
        block = lax.dynamic_slice_in_dim(
            weights, (inst_at + shift) % n_inst * inst_dev, inst_dev, 1
        )
        for m in range(inst_dev):
            coupled = coupled + block[:, m][:, None, None, None, None] * state[m]

    slabs = inst_dev * planes // n_space
    outgoing = flow_state.transpose(0, 3, 1, 2, 4).reshape(
        n_space, slabs, variables, azimuth_dev, radial
    )
    fields = lax.all_to_all(outgoing, "space", split_axis=0, concat_axis=0, tiled=True)
    fields = fields.transpose(1, 2, 0, 3, 4).reshape(slabs, variables, azimuth, radial)
    slopes = product("ivtz,rz->ivtr", fields, radial_first)
    mixed = mix(swirl_flux, fields) + mix(cross_flux, slopes)
    swirl = swirl_flow.T * radius_inverse
    turned = swirl * product("st,ivtr->ivsr", turn_first, fields)
    turned = turned + radius_inverse * product("st,ivtr->ivsr", turn_first, mixed)
    turned = turned - (viscous * radius_inverse * radius_inverse) * product(
        "st,ivtr->ivsr", turn_second, fields
    )
    turned = turned.reshape(slabs, variables, n_space, azimuth_dev, radial).transpose(2, 0, 1, 3, 4)
    turned = lax.all_to_all(turned, "space", split_axis=0, concat_axis=0, tiled=True)
    turned = turned.reshape(inst_dev, planes, variables, azimuth_dev, radial).transpose(0, 2, 3, 1, 4)

    slope = product("ivtzs,rs->ivtzr", flow_state, radial_first)
    curve = product(
        "ivtzs,rs->ivtzr", flow_state, radial_second + radius_inverse[:, None] * radial_first
    )
    upper = jnp.roll(flow_state, -1, axis=3)
    lower = jnp.roll(flow_state, 1, axis=3)
    span_slope = 0.5 * (upper - lower)
    span_curve = upper + lower - 2.0 * flow_state
    radial_part = radial_flow[:, None, :] * slope + mix(radial_flux, slope)
    radial_part = radial_part + mix(span_flux, span_slope) - viscous * (curve + span_curve)
    return turned + (coupled + radial_part)


def residual_on_device(flow_state, *rest):
    if flow_state.shape[0] * flow_state.shape[3] % lax.axis_size("space"):
        return on_device_lines(flow_state, *rest)
    return on_device(flow_state, *rest)


def solution(mesh):
    in_specs = (
        P("inst", None, "space", None, None),
        P(),
        P(),
        P("space", None),
        P(),
        P(),
        P(),
        P(),
        P(),
        P(),
        P(),
        P(),
    )
    out_specs = P("inst", None, "space", None, None)
    return jax.shard_map(
        residual_on_device, mesh=mesh, in_specs=in_specs, out_specs=out_specs, check_vma=False
    )
```

```python
import functools
import math

import jax
import jax.numpy as jnp
import numpy as np
from jax import lax
from jax.experimental import pallas as pl
from jax.experimental.pallas import tpu as pltpu
from jax.sharding import PartitionSpec as P

highest = lax.Precision.HIGHEST


def spectral(points):
    indices = jnp.arange(points)
    offsets = (indices[:, None] - indices[None, :]) % points
    spacing = 2.0 * math.pi / points
    angles = offsets.astype(jnp.float32) * (math.pi / points)
    parity = (1 - 2 * (offsets % 2)).astype(jnp.float32)
    nonzero = offsets != 0
    sines = jnp.where(nonzero, jnp.sin(angles), jnp.float32(1.0))
    first = jnp.where(nonzero, 0.5 * parity * jnp.cos(angles) / sines, jnp.float32(0.0))
    diagonal_value = -math.pi**2 / (3.0 * spacing**2) - 1.0 / 6.0
    second = jnp.where(nonzero, -0.5 * parity / (sines * sines), jnp.float32(diagonal_value))
    return (first, second)


def apply_flux(matrix, fields):
    return jnp.einsum("uv,iv...->iu...", matrix, fields, precision=highest)


def on_device_lines(
    flow_state,
    radial_first,
    radial_second,
    radial_flow,
    swirl_flow,
    radius_inverse,
    radial_flux,
    swirl_flux,
    cross_flux,
    span_flux,
    frequency,
    viscosity,
):
    inst_dev = flow_state.shape[0]
    n_inst = lax.axis_size("inst")
    n_space = lax.axis_size("space")
    instances = inst_dev * n_inst
    time_matrix, unused = spectral(instances)
    azimuth = swirl_flow.shape[1]
    radial = flow_state.shape[4]
    planes = flow_state.shape[3]
    turn_first, turn_second = spectral(azimuth)
    spacing = 2.0 * math.pi / azimuth
    turn_first = spacing * turn_first
    turn_second = spacing * spacing * turn_second
    viscous = viscosity[0]
    radial_slope = jnp.einsum("ivtzs,rs->ivtzr", flow_state, radial_first, precision=highest)
    radial_curve = jnp.einsum("ivtzs,rs->ivtzr", flow_state, radial_second, precision=highest)
    lane = math.gcd(radial, planes * radial // n_space)
    row_total = planes * radial // lane
    shape_rows = flow_state.shape[:3] + (row_total, lane)
    state_rows = flow_state.reshape(shape_rows)
    slope_rows = radial_slope.reshape(shape_rows)
    fields = lax.all_to_all(state_rows, "space", split_axis=3, concat_axis=2, tiled=True)
    slopes = lax.all_to_all(slope_rows, "space", split_axis=3, concat_axis=2, tiled=True)
    row_offset = lax.axis_index("space") * fields.shape[3]
    turning_fields = fields
    turning_slopes = slopes
    item_count = turning_fields.shape[0]
    variables = turning_fields.shape[1]
    count = turning_fields.shape[3]
    lane = turning_fields.shape[4]
    width = count * lane
    row_ids = row_offset + jnp.arange(count, dtype=jnp.int32)
    blocks = row_ids % (radial // lane)
    point_ids = (blocks[:, None] * lane + jnp.arange(lane, dtype=jnp.int32)[None, :]).reshape(width)
    inverse_tile = jnp.take(radius_inverse, point_ids)
    swirl_tile = jnp.take(swirl_flow, point_ids, axis=0).T * inverse_tile[None, :]
    turning_fields = turning_fields.reshape(item_count, variables, azimuth, width)
    turning_slopes = turning_slopes.reshape(item_count, variables, azimuth, width)
    turn_slope = jnp.einsum("st,ivtc->ivsc", turn_first, turning_fields, precision=highest)
    turn_curve = jnp.einsum("st,ivtc->ivsc", turn_second, turning_fields, precision=highest)
    cross_slope = jnp.einsum("st,ivtc->ivsc", turn_first, turning_slopes, precision=highest)
    turned_term = swirl_tile * turn_slope + inverse_tile * apply_flux(swirl_flux, turn_slope)
    turned_term = turned_term + inverse_tile * apply_flux(cross_flux, cross_slope)
    turned_term = turned_term - viscous * (inverse_tile * inverse_tile) * turn_curve
    result = lax.all_to_all(
        turned_term.reshape(item_count, variables, azimuth, count, lane),
        "space",
        split_axis=2,
        concat_axis=3,
        tiled=True,
    )
    turned = result.reshape(flow_state.shape)
    own_rows = lax.dynamic_slice_in_dim(time_matrix, lax.axis_index("inst") * inst_dev, inst_dev, 0)
    mixed_out = jnp.einsum(
        "nm,mvtzr->nvtzr",
        own_rows,
        lax.all_gather(flow_state, "inst", axis=0, tiled=True),
        precision=highest,
    )
    far_terms = frequency[0] * mixed_out + turned
    upper = jnp.roll(flow_state, -1, axis=3)
    lower = jnp.roll(flow_state, 1, axis=3)
    span_slope = 0.5 * (upper - lower)
    span_curve = upper + lower - 2.0 * flow_state
    radial_part = radial_flow[:, None, :] * radial_slope + apply_flux(radial_flux, radial_slope)
    radial_part = radial_part - viscous * (radial_curve + radius_inverse * radial_slope)
    radial_part = radial_part + apply_flux(span_flux, span_slope) - viscous * span_curve
    return far_terms + radial_part


LANE = 128
SUBLANE = 8
NT = (((1,), (1,)), ((), ()))
NN = (((1,), (0,)), ((), ()))


def spectral_table(points):
    index = np.arange(points)
    k = (index[:, None] - index[None, :]) % points
    h = 2.0 * math.pi / points
    angle = math.pi * k / points
    sign = 1.0 - 2.0 * (k % 2)
    sine = np.where(k != 0, np.sin(angle), 1.0)
    first = np.where(k != 0, 0.5 * sign * np.cos(angle) / sine, 0.0)
    second = np.where(k != 0, -0.5 * sign / sine**2, -(math.pi**2) / (3.0 * h * h) - 1.0 / 6.0)
    return first.astype(np.float32), second.astype(np.float32)


def halves(x):
    high = x.astype(jnp.bfloat16)
    return high, (x - high.astype(jnp.float32)).astype(jnp.bfloat16)


def dot3(a, b, dims):
    dot = functools.partial(
        lax.dot_general, dimension_numbers=dims, preferred_element_type=jnp.float32
    )
    return dot(a[0], b[0]) + (dot(a[0], b[1]) + dot(a[1], b[0]))


def slab_kernel(
    n_space,
    n_inst,
    time_row,
    state,
    first,
    second,
    radial_flow,
    swirl_flow,
    inverse,
    turn_high,
    turn_low,
    radial_flux,
    swirl_flux,
    cross_flux,
    span_flux,
    frequency,
    viscosity,
    out,
    outgoing,
    fields,
    turned,
    returned,
    mates,
    local,
    mixed,
    base,
    slope,
    curve,
    swirl,
    first_high,
    first_low,
    second_high,
    second_low,
    send1,
    recv1,
    send2,
    recv2,
    own_sem,
    mate_send,
    mate_recv,
):
    inst_dev, variables, azimuth_dev, planes, radial = state.shape
    azimuth = azimuth_dev * n_space
    blocks = radial // LANE
    per = SUBLANE // blocks
    chunks = variables // per
    span = azimuth_dev * SUBLANE
    me = lax.axis_index("space")
    inst_me = lax.axis_index("inst")
    order = sorted(range(1, n_space), key=lambda k: abs(2 * k - n_space))

    barrier = pltpu.get_barrier_semaphore()
    for k in order:
        pl.semaphore_signal(barrier, inc=1, device_id={"space": lax.rem(me + k, n_space)})
    for k in range(1, n_inst):
        pl.semaphore_signal(barrier, inc=1, device_id={"inst": lax.rem(inst_me + k, n_inst)})

    def at(index):
        return pl.ds(pl.multiple_of(index * span, SUBLANE), span)

    def exchange(source, target, send, recv, c, k):
        peer = lax.rem(me + k, n_space)
        return pltpu.make_async_remote_copy(
            src_ref=source.at[c, at(peer)],
            dst_ref=target.at[c, at(me)],
            send_sem=send.at[c, k],
            recv_sem=recv.at[c, k],
            device_id={"space": peer},
        )

    def own(source, target, stage, c):
        return pltpu.make_async_copy(
            source.at[c, at(me)], target.at[c, at(me)], own_sem.at[stage, c]
        )

    def mate(k):
        return pltpu.make_async_remote_copy(
            src_ref=state,
            dst_ref=mates.at[k - 1],
            send_sem=mate_send.at[k - 1],
            recv_sem=mate_recv.at[k - 1],
            device_id={"inst": lax.rem(inst_me + k, n_inst)},
        )

    def send_all(source, target, send, recv, stage, c):
        for k in order:
            exchange(source, target, send, recv, c, k).start()
        own(source, target, stage, c).start()

    def await_all(source, target, send, recv, stage, c):
        for k in order:
            exchange(source, target, send, recv, c, k).wait_recv()
        own(source, target, stage, c).wait()

    def pack(c):
        for i in range(inst_dev):
            for w in range(per):
                for t in range(azimuth_dev):
                    for b in range(blocks):
                        row = i * planes * span + t * SUBLANE + w * blocks + b
                        outgoing[c, pl.ds(row, planes, stride=span), :] = state[
                            i, c * per + w, t, :, b * LANE : (b + 1) * LANE
                        ]

    for c in range(chunks):
        pack(c)
        if c == 0:
            pl.semaphore_wait(barrier, n_space - 1 + n_inst - 1)
        send_all(outgoing, fields, send1, recv1, 0, c)
    for k in range(1, n_inst):
        mate(k).start()

    q = inverse[...]
    viscous = viscosity[0]
    first_high[...], first_low[...] = halves(first[...])
    second_high[...], second_low[...] = halves(second[...])
    first_pair = (first_high, first_low)
    second_pair = (second_high, second_low)
    swirl[...] = swirl_flow[...].T * q
    turn_rate = -viscous * q * q

    def read(pair):
        return pair[0][...], pair[1][...]

    rows = azimuth_dev * planes

    @pl.loop(0, inst_dev)
    def _(i):
        for v in range(variables):
            own_state = halves(state[i, v].reshape(rows, radial))
            slope[v] = dot3(own_state, read(first_pair), NT).reshape(azimuth_dev, planes, radial)
            curve[v] = dot3(own_state, read(second_pair), NT).reshape(azimuth_dev, planes, radial)

        @pl.loop(0, azimuth_dev)
        def _(t):
            flow_rate = radial_flow[pl.ds(t, 1), :] - viscous * q
            values = [state[i, v, t] for v in range(variables)]
            uppers = [pltpu.roll(x, planes - 1, 0) for x in values]
            lowers = [pltpu.roll(x, 1, 0) for x in values]
            steps = [0.5 * (up - low) for up, low in zip(uppers, lowers)]
            slopes = [slope[v, t] for v in range(variables)]
            for u in range(variables):
                bend = uppers[u] + lowers[u] - 2.0 * values[u]
                total = flow_rate * slopes[u] - viscous * (curve[u, t] + bend)
                for v in range(variables):
                    total = total + radial_flux[u, v] * slopes[v] + span_flux[u, v] * steps[v]
                local[i, u, t] = total

    for c in range(chunks):
        await_all(outgoing, fields, send1, recv1, 0, c)
        for w in range(per):
            v = c * per + w
            field = jnp.concatenate(
                [
                    fields[c, pl.ds(w * blocks + b, azimuth, stride=SUBLANE), :]
                    for b in range(blocks)
                ],
                axis=1,
            )
            split = halves(field)
            field_slope = dot3(split, read(first_pair), NT)
            for u in range(variables):
                term = swirl_flux[u, v] * field + cross_flux[u, v] * field_slope
                mixed[u] = mixed[u] + term if v else term
            turn = dot3((turn_high[...], turn_low[...]), split, NN)
            base[v] = swirl[...] * turn[:azimuth] + turn_rate * turn[azimuth:]

    for c in range(chunks):
        for w in range(per):
            u = c * per + w
            turn = dot3((turn_high[:azimuth], turn_low[:azimuth]), halves(mixed[u]), NN)
            total = base[u] + q * turn
            for b in range(blocks):
                turned[c, pl.ds(w * blocks + b, azimuth, stride=SUBLANE), :] = total[
                    :, b * LANE : (b + 1) * LANE
                ]
        send_all(turned, returned, send2, recv2, 1, c)

    for k in range(1, n_inst):
        mate(k).wait()
    instances = inst_dev * n_inst

    @pl.loop(0, variables)
    def _(v):
        @pl.loop(0, azimuth_dev)
        def _(t):
            for n in range(inst_dev):
                total = local[n, v, t]
                for k in range(n_inst):
                    for m in range(inst_dev):
                        offset = (n - m + k * inst_dev) % instances
                        value = state[m, v, t] if k == 0 else mates[k - 1, m, v, t]
                        total = total + (frequency[0] * time_row[offset]) * value
                local[n, v, t] = total

    for c in range(chunks):
        await_all(turned, returned, send2, recv2, 1, c)
        for i in range(inst_dev):
            for w in range(per):
                for t in range(azimuth_dev):
                    for b in range(blocks):
                        row = i * planes * span + t * SUBLANE + w * blocks + b
                        lanes = slice(b * LANE, (b + 1) * LANE)
                        out[i, c * per + w, t, :, lanes] = (
                            local[i, c * per + w, t, :, lanes]
                            + returned[c, pl.ds(row, planes, stride=span), :]
                        )
    for c in range(chunks):
        for k in order:
            exchange(outgoing, fields, send1, recv1, c, k).wait_send()
            exchange(turned, returned, send2, recv2, c, k).wait_send()


def on_device(
    flow_state,
    radial_first,
    radial_second,
    radial_flow,
    swirl_flow,
    radius_inverse,
    radial_flux,
    swirl_flux,
    cross_flux,
    span_flux,
    frequency,
    viscosity,
):
    inst_dev, variables, azimuth_dev, planes, radial = flow_state.shape
    n_inst = lax.axis_size("inst")
    n_space = lax.axis_size("space")
    azimuth = swirl_flow.shape[1]
    blocks = radial // LANE
    chunks = variables * blocks // SUBLANE
    time_row = [float(x) for x in spectral_table(inst_dev * n_inst)[0][:, 0]]
    turn_first, turn_second = spectral_table(azimuth)
    h = np.float32(2.0 * math.pi / azimuth)
    turn = np.concatenate([h * turn_first, h * h * turn_second])
    turn_high = turn.astype(jnp.bfloat16)
    turn_low = (turn - turn_high.astype(np.float32)).astype(jnp.bfloat16)
    vmem = pl.BlockSpec(memory_space=pltpu.VMEM)
    smem = pl.BlockSpec(memory_space=pltpu.SMEM)
    packed = pltpu.VMEM((chunks, n_space * azimuth_dev * SUBLANE, LANE), jnp.float32)
    slab = pltpu.VMEM((variables, azimuth, radial), jnp.float32)
    pencil = pltpu.VMEM((variables, azimuth_dev, planes, radial), jnp.float32)
    square = pltpu.VMEM((radial, radial), jnp.bfloat16)
    sems = pltpu.SemaphoreType.DMA((chunks, n_space))
    return pl.pallas_call(
        functools.partial(slab_kernel, n_space, n_inst, time_row),
        out_shape=jax.ShapeDtypeStruct(flow_state.shape, jnp.float32),
        in_specs=[vmem] * 8 + [smem] * 6,
        out_specs=vmem,
        scratch_shapes=[
            packed,
            packed,
            packed,
            packed,
            pltpu.VMEM((n_inst - 1,) + flow_state.shape, jnp.float32),
            pltpu.VMEM(flow_state.shape, jnp.float32),
            slab,
            slab,
            pencil,
            pencil,
            pltpu.VMEM((azimuth, radial), jnp.float32),
            square,
            square,
            square,
            square,
            sems,
            sems,
            sems,
            sems,
            pltpu.SemaphoreType.DMA((2, chunks)),
            pltpu.SemaphoreType.DMA((n_inst - 1,)),
            pltpu.SemaphoreType.DMA((n_inst - 1,)),
        ],
        compiler_params=pltpu.CompilerParams(
            collective_id=0, has_side_effects=True, vmem_limit_bytes=56 * 1024 * 1024
        ),
    )(
        flow_state,
        radial_first,
        radial_second,
        radial_flow,
        swirl_flow,
        radius_inverse.reshape(1, radial),
        jnp.asarray(turn_high),
        jnp.asarray(turn_low),
        radial_flux,
        swirl_flux,
        cross_flux,
        span_flux,
        frequency,
        viscosity,
    )


def residual_on_device(flow_state, *rest):
    inst_dev, variables, azimuth_dev, planes, radial = flow_state.shape
    blocks = radial // LANE
    slabs = (
        inst_dev * planes == lax.axis_size("space")
        and lax.axis_size("inst") > 1
        and planes == SUBLANE
        and radial == blocks * LANE
        and SUBLANE % blocks == 0
        and variables * blocks % SUBLANE == 0
    )
    return (on_device if slabs else on_device_lines)(flow_state, *rest)


def solution(mesh):
    in_specs = (
        P("inst", None, "space", None, None),
        P(),
        P(),
        P("space", None),
        P(),
        P(),
        P(),
        P(),
        P(),
        P(),
        P(),
        P(),
    )
    out_specs = P("inst", None, "space", None, None)
    return jax.shard_map(
        residual_on_device, mesh=mesh, in_specs=in_specs, out_specs=out_specs, check_vma=False
    )
```

```python
import functools
import math

import jax
import jax.numpy as jnp
import numpy as np
from jax import lax
from jax.experimental import pallas as pl
from jax.experimental.pallas import tpu as pltpu
from jax.sharding import PartitionSpec as P

highest = lax.Precision.HIGHEST


def spectral(points):
    indices = jnp.arange(points)
    offsets = (indices[:, None] - indices[None, :]) % points
    spacing = 2.0 * math.pi / points
    angles = offsets.astype(jnp.float32) * (math.pi / points)
    parity = (1 - 2 * (offsets % 2)).astype(jnp.float32)
    nonzero = offsets != 0
    sines = jnp.where(nonzero, jnp.sin(angles), jnp.float32(1.0))
    first = jnp.where(nonzero, 0.5 * parity * jnp.cos(angles) / sines, jnp.float32(0.0))
    diagonal_value = -math.pi**2 / (3.0 * spacing**2) - 1.0 / 6.0
    second = jnp.where(nonzero, -0.5 * parity / (sines * sines), jnp.float32(diagonal_value))
    return (first, second)


def apply_flux(matrix, fields):
    return jnp.einsum("uv,iv...->iu...", matrix, fields, precision=highest)


def on_device_lines(
    flow_state,
    radial_first,
    radial_second,
    radial_flow,
    swirl_flow,
    radius_inverse,
    radial_flux,
    swirl_flux,
    cross_flux,
    span_flux,
    frequency,
    viscosity,
):
    inst_dev = flow_state.shape[0]
    n_inst = lax.axis_size("inst")
    n_space = lax.axis_size("space")
    instances = inst_dev * n_inst
    time_matrix, unused = spectral(instances)
    azimuth = swirl_flow.shape[1]
    radial = flow_state.shape[4]
    planes = flow_state.shape[3]
    turn_first, turn_second = spectral(azimuth)
    spacing = 2.0 * math.pi / azimuth
    turn_first = spacing * turn_first
    turn_second = spacing * spacing * turn_second
    viscous = viscosity[0]
    radial_slope = jnp.einsum("ivtzs,rs->ivtzr", flow_state, radial_first, precision=highest)
    radial_curve = jnp.einsum("ivtzs,rs->ivtzr", flow_state, radial_second, precision=highest)
    lane = math.gcd(radial, planes * radial // n_space)
    row_total = planes * radial // lane
    shape_rows = flow_state.shape[:3] + (row_total, lane)
    state_rows = flow_state.reshape(shape_rows)
    slope_rows = radial_slope.reshape(shape_rows)
    fields = lax.all_to_all(state_rows, "space", split_axis=3, concat_axis=2, tiled=True)
    slopes = lax.all_to_all(slope_rows, "space", split_axis=3, concat_axis=2, tiled=True)
    row_offset = lax.axis_index("space") * fields.shape[3]
    turning_fields = fields
    turning_slopes = slopes
    item_count = turning_fields.shape[0]
    variables = turning_fields.shape[1]
    count = turning_fields.shape[3]
    lane = turning_fields.shape[4]
    width = count * lane
    row_ids = row_offset + jnp.arange(count, dtype=jnp.int32)
    blocks = row_ids % (radial // lane)
    point_ids = (blocks[:, None] * lane + jnp.arange(lane, dtype=jnp.int32)[None, :]).reshape(width)
    inverse_tile = jnp.take(radius_inverse, point_ids)
    swirl_tile = jnp.take(swirl_flow, point_ids, axis=0).T * inverse_tile[None, :]
    turning_fields = turning_fields.reshape(item_count, variables, azimuth, width)
    turning_slopes = turning_slopes.reshape(item_count, variables, azimuth, width)
    turn_slope = jnp.einsum("st,ivtc->ivsc", turn_first, turning_fields, precision=highest)
    turn_curve = jnp.einsum("st,ivtc->ivsc", turn_second, turning_fields, precision=highest)
    cross_slope = jnp.einsum("st,ivtc->ivsc", turn_first, turning_slopes, precision=highest)
    turned_term = swirl_tile * turn_slope + inverse_tile * apply_flux(swirl_flux, turn_slope)
    turned_term = turned_term + inverse_tile * apply_flux(cross_flux, cross_slope)
    turned_term = turned_term - viscous * (inverse_tile * inverse_tile) * turn_curve
    result = lax.all_to_all(
        turned_term.reshape(item_count, variables, azimuth, count, lane),
        "space",
        split_axis=2,
        concat_axis=3,
        tiled=True,
    )
    turned = result.reshape(flow_state.shape)
    own_rows = lax.dynamic_slice_in_dim(time_matrix, lax.axis_index("inst") * inst_dev, inst_dev, 0)
    mixed_out = jnp.einsum(
        "nm,mvtzr->nvtzr",
        own_rows,
        lax.all_gather(flow_state, "inst", axis=0, tiled=True),
        precision=highest,
    )
    far_terms = frequency[0] * mixed_out + turned
    upper = jnp.roll(flow_state, -1, axis=3)
    lower = jnp.roll(flow_state, 1, axis=3)
    span_slope = 0.5 * (upper - lower)
    span_curve = upper + lower - 2.0 * flow_state
    radial_part = radial_flow[:, None, :] * radial_slope + apply_flux(radial_flux, radial_slope)
    radial_part = radial_part - viscous * (radial_curve + radius_inverse * radial_slope)
    radial_part = radial_part + apply_flux(span_flux, span_slope) - viscous * span_curve
    return far_terms + radial_part


LANE = 128
SUBLANE = 8
NT = (((1,), (1,)), ((), ()))
NN = (((1,), (0,)), ((), ()))


def spectral_table(points):
    index = np.arange(points)
    k = (index[:, None] - index[None, :]) % points
    h = 2.0 * math.pi / points
    angle = math.pi * k / points
    sign = 1.0 - 2.0 * (k % 2)
    sine = np.where(k != 0, np.sin(angle), 1.0)
    first = np.where(k != 0, 0.5 * sign * np.cos(angle) / sine, 0.0)
    second = np.where(k != 0, -0.5 * sign / sine**2, -(math.pi**2) / (3.0 * h * h) - 1.0 / 6.0)
    return first.astype(np.float32), second.astype(np.float32)


def halves(x):
    high = x.astype(jnp.bfloat16)
    return high, (x - high.astype(jnp.float32)).astype(jnp.bfloat16)


def dot3(a, b, dims):
    dot = functools.partial(
        lax.dot_general, dimension_numbers=dims, preferred_element_type=jnp.float32
    )
    return dot(a[0], b[0]) + (dot(a[0], b[1]) + dot(a[1], b[0]))


def slab_kernel(
    n_space,
    n_inst,
    time_row,
    state_in,
    first_in,
    second_in,
    swirl_in,
    radial_flow,
    inverse,
    turn_high,
    turn_low,
    radial_flux,
    swirl_flux,
    cross_flux,
    span_flux,
    frequency,
    viscosity,
    out,
    state,
    first,
    second,
    outgoing,
    fields,
    turned,
    returned,
    mates,
    local,
    mixed,
    base,
    slope,
    curve,
    swirl,
    first_high,
    first_low,
    second_high,
    second_low,
    last_high,
    last_low,
    send1,
    recv1,
    send2,
    recv2,
    own_sem,
    mate_send,
    mate_recv,
    load_sem,
):
    inst_dev, variables, azimuth_dev, planes, radial = state.shape
    azimuth = azimuth_dev * n_space
    blocks = radial // LANE
    chunks = variables
    span = azimuth_dev * blocks
    me = lax.axis_index("space")
    inst_me = lax.axis_index("inst")
    half = n_space // 2
    quarter = max(n_space // 4, 1)
    upper_half = me // half
    depth = upper_half * (n_space - 1 - me) + (1 - upper_half) * me
    shift = (depth // quarter) % 2 * (quarter - 1)
    heading = 1 - 2 * upper_half
    others = range(1, n_space)

    def load_state(c):
        return pltpu.make_async_copy(state_in.at[:, c], state.at[:, c], load_sem.at[c])

    loads = [
        pltpu.make_async_copy(source, target, load_sem.at[variables + n])
        for n, (source, target) in enumerate(
            [(first_in, first), (second_in, second), (swirl_in, swirl)]
        )
    ]
    for c in range(chunks):
        load_state(c).start()
    for load in loads:
        load.start()

    barrier = pltpu.get_barrier_semaphore()
    for k in others:
        pl.semaphore_signal(barrier, inc=1, device_id={"space": lax.rem(me + k, n_space)})
    for k in range(1, n_inst):
        pl.semaphore_signal(barrier, inc=1, device_id={"inst": lax.rem(inst_me + k, n_inst)})

    def at(index):
        return pl.ds(pl.multiple_of(index * span, SUBLANE), span)

    def exchange(source, target, send, recv, c, k):
        step = 1 + lax.rem(k - 1 + shift, n_space - 1)
        peer = lax.rem(me + heading * step + n_space, n_space)
        return pltpu.make_async_remote_copy(
            src_ref=source.at[c, at(peer)],
            dst_ref=target.at[c, at(me)],
            send_sem=send.at[c, k],
            recv_sem=recv.at[c, me],
            device_id={"space": peer},
        )

    def own(source, target, stage, c):
        return pltpu.make_async_copy(
            source.at[c, at(me)], target.at[c, at(me)], own_sem.at[stage, c]
        )

    def mate(k):
        return pltpu.make_async_remote_copy(
            src_ref=state,
            dst_ref=mates.at[k - 1],
            send_sem=mate_send.at[k - 1],
            recv_sem=mate_recv.at[k - 1],
            device_id={"inst": lax.rem(inst_me + k, n_inst)},
        )

    def send_all(source, target, send, recv, stage, c):
        for k in others:
            exchange(source, target, send, recv, c, k).start()
        own(source, target, stage, c).start()

    def await_all(source, target, send, recv, stage, c):
        for k in others:
            peer = lax.rem(me + k, n_space)
            pltpu.make_async_remote_copy(
                src_ref=source.at[c, at(peer)],
                dst_ref=target.at[c, at(peer)],
                send_sem=send.at[c, k],
                recv_sem=recv.at[c, peer],
                device_id={"space": peer},
            ).wait_recv()
        own(source, target, stage, c).wait()

    def pack(c):
        for i in range(inst_dev):
            for at_row in range(azimuth_dev * blocks):
                step, block = divmod(at_row, blocks)
                row = i * planes * span + at_row
                outgoing[c, pl.ds(row, planes, stride=span), :] = state[
                    i, c, step, :, block * LANE : (block + 1) * LANE
                ]

    for c in range(chunks):
        load_state(c).wait()
        pack(c)
        if c == 0:
            pl.semaphore_wait(barrier, n_space - 1 + n_inst - 1)
        send_all(outgoing, fields, send1, recv1, 0, c)
    for k in range(1, n_inst):
        mate(k).start()

    q = inverse[...]
    viscous = viscosity[0]
    for load in loads:
        load.wait()
    first_high[...], first_low[...] = halves(first[...])
    second_high[...], second_low[...] = halves(second[...])
    first_pair = (first_high, first_low)
    second_pair = (second_high, second_low)
    swirl[...] = swirl[...] * q
    turn_rate = -viscous * q * q

    def read(pair):
        return pair[0][...], pair[1][...]

    rows = azimuth_dev * planes

    @pl.loop(0, inst_dev)
    def _(i):
        for v in range(variables):
            own_state = halves(state[i, v].reshape(rows, radial))
            slope[v] = dot3(own_state, read(first_pair), NT).reshape(azimuth_dev, planes, radial)
            curve[v] = dot3(own_state, read(second_pair), NT).reshape(azimuth_dev, planes, radial)

        @pl.loop(0, azimuth_dev)
        def _(t):
            flow_rate = radial_flow[pl.ds(t, 1), :] - viscous * q
            values = [state[i, v, t] for v in range(variables)]
            uppers = [pltpu.roll(x, planes - 1, 0) for x in values]
            lowers = [pltpu.roll(x, 1, 0) for x in values]
            steps = [0.5 * (up - low) for up, low in zip(uppers, lowers)]
            slopes = [slope[v, t] for v in range(variables)]
            for u in range(variables):
                bend = uppers[u] + lowers[u] - 2.0 * values[u]
                total = flow_rate * slopes[u] - viscous * (curve[u, t] + bend)
                for v in range(variables):
                    total = total + radial_flux[u, v] * slopes[v] + span_flux[u, v] * steps[v]
                local[i, u, t] = total

    def turn_base(v, split):
        turn = dot3((turn_high[...], turn_low[...]), split, NN)
        base[v] = swirl[...] * turn[:azimuth] + turn_rate * turn[azimuth:]

    for v in range(variables):
        await_all(outgoing, fields, send1, recv1, 0, v)
        field = jnp.concatenate(
            [fields[v, pl.ds(b, azimuth, stride=blocks), :] for b in range(blocks)], axis=1
        )
        split = halves(field)
        field_slope = dot3(split, read(first_pair), NT)
        if v < variables - 1:
            turn_base(v, split)
        else:
            last_high[...], last_low[...] = split
        for u in range(variables):
            term = swirl_flux[u, v] * field + cross_flux[u, v] * field_slope
            mixed[u] = mixed[u] + term if v else term

    for u in range(variables):
        if u == variables - 1:
            turn_base(u, (last_high[...], last_low[...]))
        turn = dot3((turn_high[:azimuth], turn_low[:azimuth]), halves(mixed[u]), NN)
        total = base[u] + q * turn
        for b in range(blocks):
            turned[u, pl.ds(b, azimuth, stride=blocks), :] = total[:, b * LANE : (b + 1) * LANE]
        send_all(turned, returned, send2, recv2, 1, u)

    for k in range(1, n_inst):
        mate(k).wait()
    instances = inst_dev * n_inst

    @pl.loop(0, variables)
    def _(v):
        @pl.loop(0, azimuth_dev)
        def _(t):
            for n in range(inst_dev):
                total = local[n, v, t]
                for k in range(n_inst):
                    for m in range(inst_dev):
                        offset = (n - m + k * inst_dev) % instances
                        value = state[m, v, t] if k == 0 else mates[k - 1, m, v, t]
                        total = total + (frequency[0] * time_row[offset]) * value
                local[n, v, t] = total

    for c in range(chunks):
        await_all(turned, returned, send2, recv2, 1, c)
        for i in range(inst_dev):
            for at_row in range(azimuth_dev * blocks):
                step, block = divmod(at_row, blocks)
                row = i * planes * span + at_row
                lanes = slice(block * LANE, (block + 1) * LANE)
                out[i, c, step, :, lanes] = (
                    local[i, c, step, :, lanes]
                    + returned[c, pl.ds(row, planes, stride=span), :]
                )
    for c in range(chunks):
        for k in others:
            exchange(outgoing, fields, send1, recv1, c, k).wait_send()
            exchange(turned, returned, send2, recv2, c, k).wait_send()


def on_device(
    flow_state,
    radial_first,
    radial_second,
    radial_flow,
    swirl_flow,
    radius_inverse,
    radial_flux,
    swirl_flux,
    cross_flux,
    span_flux,
    frequency,
    viscosity,
):
    inst_dev, variables, azimuth_dev, planes, radial = flow_state.shape
    n_inst = lax.axis_size("inst")
    n_space = lax.axis_size("space")
    azimuth = swirl_flow.shape[1]
    blocks = radial // LANE
    time_row = [float(x) for x in spectral_table(inst_dev * n_inst)[0][:, 0]]
    turn_first, turn_second = spectral_table(azimuth)
    h = np.float32(2.0 * math.pi / azimuth)
    turn = np.concatenate([h * turn_first, h * h * turn_second])
    turn_high = turn.astype(jnp.bfloat16)
    turn_low = (turn - turn_high.astype(np.float32)).astype(jnp.bfloat16)
    vmem = pl.BlockSpec(memory_space=pltpu.VMEM)
    hbm = pl.BlockSpec(memory_space=pltpu.HBM)
    smem = pl.BlockSpec(memory_space=pltpu.SMEM)
    packed = pltpu.VMEM((variables, azimuth * blocks, LANE), jnp.float32)
    slab = pltpu.VMEM((variables, azimuth, radial), jnp.float32)
    pencil = pltpu.VMEM((variables, azimuth_dev, planes, radial), jnp.float32)
    half_slab = pltpu.VMEM((azimuth, radial), jnp.bfloat16)
    square = pltpu.VMEM((radial, radial), jnp.bfloat16)
    sems = pltpu.SemaphoreType.DMA((variables, n_space))
    return pl.pallas_call(
        functools.partial(slab_kernel, n_space, n_inst, time_row),
        out_shape=pltpu.VMEM(flow_state.shape, jnp.float32),
        in_specs=[hbm] * 4 + [vmem] * 4 + [smem] * 6,
        out_specs=vmem,
        scratch_shapes=[
            pltpu.VMEM(flow_state.shape, jnp.float32),
            pltpu.VMEM((radial, radial), jnp.float32),
            pltpu.VMEM((radial, radial), jnp.float32),
            packed,
            packed,
            packed,
            packed,
            pltpu.VMEM((n_inst - 1,) + flow_state.shape, jnp.float32),
            pltpu.VMEM(flow_state.shape, jnp.float32),
            slab,
            slab,
            pencil,
            pencil,
            pltpu.VMEM((azimuth, radial), jnp.float32),
            square,
            square,
            square,
            square,
            half_slab,
            half_slab,
            sems,
            sems,
            sems,
            sems,
            pltpu.SemaphoreType.DMA((2, variables)),
            pltpu.SemaphoreType.DMA((n_inst - 1,)),
            pltpu.SemaphoreType.DMA((n_inst - 1,)),
            pltpu.SemaphoreType.DMA((variables + 3,)),
        ],
        compiler_params=pltpu.CompilerParams(
            collective_id=0, has_side_effects=True, vmem_limit_bytes=59 * 1024 * 1024
        ),
    )(
        flow_state,
        radial_first,
        radial_second,
        swirl_flow.T,
        radial_flow,
        radius_inverse.reshape(1, radial),
        jnp.asarray(turn_high),
        jnp.asarray(turn_low),
        radial_flux,
        swirl_flux,
        cross_flux,
        span_flux,
        frequency,
        viscosity,
    )


def residual_on_device(flow_state, *rest):
    inst_dev, variables, azimuth_dev, planes, radial = flow_state.shape
    blocks = radial // LANE
    slabs = (
        inst_dev * planes == lax.axis_size("space")
        and lax.axis_size("inst") > 1
        and planes == SUBLANE
        and radial == blocks * LANE
        and azimuth_dev * blocks % SUBLANE == 0
    )
    return (on_device if slabs else on_device_lines)(flow_state, *rest)


def solution(mesh):
    in_specs = (
        P("inst", None, "space", None, None),
        P(),
        P(),
        P("space", None),
        P(),
        P(),
        P(),
        P(),
        P(),
        P(),
        P(),
        P(),
    )
    out_specs = P("inst", None, "space", None, None)
    return jax.shard_map(
        residual_on_device, mesh=mesh, in_specs=in_specs, out_specs=out_specs, check_vma=False
    )
```

```python
import functools
import math

import jax
import jax.numpy as jnp
import numpy as np
from jax import lax
from jax.experimental import pallas as pl
from jax.experimental.pallas import tpu as pltpu
from jax.sharding import PartitionSpec as P

highest = lax.Precision.HIGHEST


def spectral(points):
    indices = jnp.arange(points)
    offsets = (indices[:, None] - indices[None, :]) % points
    spacing = 2.0 * math.pi / points
    angles = offsets.astype(jnp.float32) * (math.pi / points)
    parity = (1 - 2 * (offsets % 2)).astype(jnp.float32)
    nonzero = offsets != 0
    sines = jnp.where(nonzero, jnp.sin(angles), jnp.float32(1.0))
    first = jnp.where(nonzero, 0.5 * parity * jnp.cos(angles) / sines, jnp.float32(0.0))
    diagonal_value = -math.pi**2 / (3.0 * spacing**2) - 1.0 / 6.0
    second = jnp.where(nonzero, -0.5 * parity / (sines * sines), jnp.float32(diagonal_value))
    return (first, second)


def apply_flux(matrix, fields):
    return jnp.einsum("uv,iv...->iu...", matrix, fields, precision=highest)


def on_device_lines(
    flow_state,
    radial_first,
    radial_second,
    radial_flow,
    swirl_flow,
    radius_inverse,
    radial_flux,
    swirl_flux,
    cross_flux,
    span_flux,
    frequency,
    viscosity,
):
    inst_dev = flow_state.shape[0]
    n_inst = lax.axis_size("inst")
    n_space = lax.axis_size("space")
    instances = inst_dev * n_inst
    time_matrix, unused = spectral(instances)
    azimuth = swirl_flow.shape[1]
    radial = flow_state.shape[4]
    planes = flow_state.shape[3]
    turn_first, turn_second = spectral(azimuth)
    spacing = 2.0 * math.pi / azimuth
    turn_first = spacing * turn_first
    turn_second = spacing * spacing * turn_second
    viscous = viscosity[0]
    radial_slope = jnp.einsum("ivtzs,rs->ivtzr", flow_state, radial_first, precision=highest)
    radial_curve = jnp.einsum("ivtzs,rs->ivtzr", flow_state, radial_second, precision=highest)
    lane = math.gcd(radial, planes * radial // n_space)
    row_total = planes * radial // lane
    shape_rows = flow_state.shape[:3] + (row_total, lane)
    state_rows = flow_state.reshape(shape_rows)
    slope_rows = radial_slope.reshape(shape_rows)
    fields = lax.all_to_all(state_rows, "space", split_axis=3, concat_axis=2, tiled=True)
    slopes = lax.all_to_all(slope_rows, "space", split_axis=3, concat_axis=2, tiled=True)
    row_offset = lax.axis_index("space") * fields.shape[3]
    turning_fields = fields
    turning_slopes = slopes
    item_count = turning_fields.shape[0]
    variables = turning_fields.shape[1]
    count = turning_fields.shape[3]
    lane = turning_fields.shape[4]
    width = count * lane
    row_ids = row_offset + jnp.arange(count, dtype=jnp.int32)
    blocks = row_ids % (radial // lane)
    point_ids = (blocks[:, None] * lane + jnp.arange(lane, dtype=jnp.int32)[None, :]).reshape(width)
    inverse_tile = jnp.take(radius_inverse, point_ids)
    swirl_tile = jnp.take(swirl_flow, point_ids, axis=0).T * inverse_tile[None, :]
    turning_fields = turning_fields.reshape(item_count, variables, azimuth, width)
    turning_slopes = turning_slopes.reshape(item_count, variables, azimuth, width)
    turn_slope = jnp.einsum("st,ivtc->ivsc", turn_first, turning_fields, precision=highest)
    turn_curve = jnp.einsum("st,ivtc->ivsc", turn_second, turning_fields, precision=highest)
    cross_slope = jnp.einsum("st,ivtc->ivsc", turn_first, turning_slopes, precision=highest)
    turned_term = swirl_tile * turn_slope + inverse_tile * apply_flux(swirl_flux, turn_slope)
    turned_term = turned_term + inverse_tile * apply_flux(cross_flux, cross_slope)
    turned_term = turned_term - viscous * (inverse_tile * inverse_tile) * turn_curve
    result = lax.all_to_all(
        turned_term.reshape(item_count, variables, azimuth, count, lane),
        "space",
        split_axis=2,
        concat_axis=3,
        tiled=True,
    )
    turned = result.reshape(flow_state.shape)
    own_rows = lax.dynamic_slice_in_dim(time_matrix, lax.axis_index("inst") * inst_dev, inst_dev, 0)
    mixed_out = jnp.einsum(
        "nm,mvtzr->nvtzr",
        own_rows,
        lax.all_gather(flow_state, "inst", axis=0, tiled=True),
        precision=highest,
    )
    far_terms = frequency[0] * mixed_out + turned
    upper = jnp.roll(flow_state, -1, axis=3)
    lower = jnp.roll(flow_state, 1, axis=3)
    span_slope = 0.5 * (upper - lower)
    span_curve = upper + lower - 2.0 * flow_state
    radial_part = radial_flow[:, None, :] * radial_slope + apply_flux(radial_flux, radial_slope)
    radial_part = radial_part - viscous * (radial_curve + radius_inverse * radial_slope)
    radial_part = radial_part + apply_flux(span_flux, span_slope) - viscous * span_curve
    return far_terms + radial_part


LANE = 128
SUBLANE = 8
NT = (((1,), (1,)), ((), ()))
NN = (((1,), (0,)), ((), ()))


def spectral_table(points):
    index = np.arange(points)
    k = (index[:, None] - index[None, :]) % points
    h = 2.0 * math.pi / points
    angle = math.pi * k / points
    sign = 1.0 - 2.0 * (k % 2)
    sine = np.where(k != 0, np.sin(angle), 1.0)
    first = np.where(k != 0, 0.5 * sign * np.cos(angle) / sine, 0.0)
    second = np.where(k != 0, -0.5 * sign / sine**2, -(math.pi**2) / (3.0 * h * h) - 1.0 / 6.0)
    return first.astype(np.float32), second.astype(np.float32)


def halves(x):
    high = x.astype(jnp.bfloat16)
    return high, (x - high.astype(jnp.float32)).astype(jnp.bfloat16)


def dot3(a, b, dims):
    dot = functools.partial(
        lax.dot_general, dimension_numbers=dims, preferred_element_type=jnp.float32
    )
    return dot(a[0], b[0]) + (dot(a[0], b[1]) + dot(a[1], b[0]))


def slab_kernel(
    n_space,
    n_inst,
    time_row,
    state_in,
    first_in,
    second_in,
    swirl_in,
    radial_flow,
    inverse,
    turn_high,
    turn_low,
    radial_flux,
    swirl_flux,
    cross_flux,
    span_flux,
    frequency,
    viscosity,
    out,
    state,
    first,
    second,
    outgoing,
    fields,
    turned,
    returned,
    mates,
    local,
    mixed,
    base,
    slope,
    curve,
    swirl,
    first_high,
    first_low,
    second_high,
    second_low,
    last_high,
    last_low,
    send1,
    recv1,
    send2,
    recv2,
    own_sem,
    mate_send,
    mate_recv,
    load_sem,
):
    inst_dev, variables, azimuth_dev, planes, radial = state.shape
    azimuth = azimuth_dev * n_space
    blocks = radial // LANE
    chunks = variables
    span = azimuth_dev * blocks
    me = lax.axis_index("space")
    inst_me = lax.axis_index("inst")
    pairs = n_space // 2
    pair, side = me // 2, lax.rem(me, 2)
    quarter = max(pairs // 4, 1)
    upper_half = pair // max(pairs // 2, 1)
    depth = upper_half * (pairs - 1 - pair) + (1 - upper_half) * pair
    shift = (depth // quarter) % 2 * (quarter - 1)
    heading = 1 - 2 * upper_half
    routes = [(step, core) for core in range(2) for step in range(1, pairs)]
    others = range(1, n_space)

    def load_state(c):
        return pltpu.make_async_copy(state_in.at[:, c], state.at[:, c], load_sem.at[c])

    loads = [
        pltpu.make_async_copy(source, target, load_sem.at[variables + n])
        for n, (source, target) in enumerate(
            [(first_in, first), (second_in, second), (swirl_in, swirl)]
        )
    ]
    for c in range(chunks):
        load_state(c).start()
    for load in loads:
        load.start()

    barrier = pltpu.get_barrier_semaphore()
    for k in others:
        pl.semaphore_signal(barrier, inc=1, device_id={"space": lax.rem(me + k, n_space)})
    for k in range(1, n_inst):
        pl.semaphore_signal(barrier, inc=1, device_id={"inst": lax.rem(inst_me + k, n_inst)})

    def at(index):
        return pl.ds(pl.multiple_of(index * span, SUBLANE), span)

    def exchange(source, target, send, recv, c, route):
        step, core = route
        if step:
            step = 1 + lax.rem(step - 1 + shift, pairs - 1)
            peer = 2 * lax.rem(pair + heading * step + pairs, pairs) + core
        else:
            peer = 2 * pair + 1 - side
        k = 2 * route[0] + core
        return pltpu.make_async_remote_copy(
            src_ref=source.at[c, at(peer)],
            dst_ref=target.at[c, at(me)],
            send_sem=send.at[c, k],
            recv_sem=recv.at[c, me],
            device_id={"space": peer},
        )

    def own(source, target, stage, c):
        return pltpu.make_async_copy(
            source.at[c, at(me)], target.at[c, at(me)], own_sem.at[stage, c]
        )

    def mate(k):
        return pltpu.make_async_remote_copy(
            src_ref=state,
            dst_ref=mates.at[k - 1],
            send_sem=mate_send.at[k - 1],
            recv_sem=mate_recv.at[k - 1],
            device_id={"inst": lax.rem(inst_me + k, n_inst)},
        )

    def send_side(source, target, send, recv, stage, c, core):
        for route in routes:
            if route[1] == core:
                exchange(source, target, send, recv, c, route).start()
        if core == 0:
            exchange(source, target, send, recv, c, (0, 0)).start()
            own(source, target, stage, c).start()

    def send_all(source, target, send, recv, stage, c):
        for core in range(2):
            send_side(source, target, send, recv, stage, c, core)

    def await_all(source, target, send, recv, stage, c):
        for k in others:
            peer = lax.rem(me + k, n_space)
            pltpu.make_async_remote_copy(
                src_ref=source.at[c, at(peer)],
                dst_ref=target.at[c, at(peer)],
                send_sem=send.at[c, k],
                recv_sem=recv.at[c, peer],
                device_id={"space": peer},
            ).wait_recv()
        own(source, target, stage, c).wait()

    def pack(c):
        for i in range(inst_dev):
            for at_row in range(azimuth_dev * blocks):
                step, block = divmod(at_row, blocks)
                row = i * planes * span + at_row
                outgoing[c, pl.ds(row, planes, stride=span), :] = state[
                    i, c, step, :, block * LANE : (block + 1) * LANE
                ]

    for c in range(chunks):
        load_state(c).wait()
        pack(c)
        if c == 0:
            pl.semaphore_wait(barrier, n_space - 1 + n_inst - 1)
        send_side(outgoing, fields, send1, recv1, 0, c, 0)
    for c in range(chunks):
        send_side(outgoing, fields, send1, recv1, 0, c, 1)
    for k in range(1, n_inst):
        mate(k).start()

    q = inverse[...]
    viscous = viscosity[0]
    for load in loads:
        load.wait()
    first_high[...], first_low[...] = halves(first[...])
    second_high[...], second_low[...] = halves(second[...])
    first_pair = (first_high, first_low)
    second_pair = (second_high, second_low)
    swirl[...] = swirl[...] * q
    turn_rate = -viscous * q * q

    def read(pair):
        return pair[0][...], pair[1][...]

    rows = azimuth_dev * planes

    @pl.loop(0, inst_dev)
    def _(i):
        for v in range(variables):
            own_state = halves(state[i, v].reshape(rows, radial))
            slope[v] = dot3(own_state, read(first_pair), NT).reshape(azimuth_dev, planes, radial)
            curve[v] = dot3(own_state, read(second_pair), NT).reshape(azimuth_dev, planes, radial)

        @pl.loop(0, azimuth_dev)
        def _(t):
            flow_rate = radial_flow[pl.ds(t, 1), :] - viscous * q
            values = [state[i, v, t] for v in range(variables)]
            uppers = [pltpu.roll(x, planes - 1, 0) for x in values]
            lowers = [pltpu.roll(x, 1, 0) for x in values]
            steps = [0.5 * (up - low) for up, low in zip(uppers, lowers)]
            slopes = [slope[v, t] for v in range(variables)]
            for u in range(variables):
                bend = uppers[u] + lowers[u] - 2.0 * values[u]
                total = flow_rate * slopes[u] - viscous * (curve[u, t] + bend)
                for v in range(variables):
                    total = total + radial_flux[u, v] * slopes[v] + span_flux[u, v] * steps[v]
                local[i, u, t] = total

    def turn_base(v, split):
        turn = dot3((turn_high[...], turn_low[...]), split, NN)
        base[v] = swirl[...] * turn[:azimuth] + turn_rate * turn[azimuth:]

    for v in range(variables):
        await_all(outgoing, fields, send1, recv1, 0, v)
        field = jnp.concatenate(
            [fields[v, pl.ds(b, azimuth, stride=blocks), :] for b in range(blocks)], axis=1
        )
        split = halves(field)
        field_slope = dot3(split, read(first_pair), NT)
        if v < variables - 1:
            turn_base(v, split)
        else:
            last_high[...], last_low[...] = split
        for u in range(variables):
            term = swirl_flux[u, v] * field + cross_flux[u, v] * field_slope
            mixed[u] = mixed[u] + term if v else term

    for u in range(variables):
        if u == variables - 1:
            turn_base(u, (last_high[...], last_low[...]))
        turn = dot3((turn_high[:azimuth], turn_low[:azimuth]), halves(mixed[u]), NN)
        total = base[u] + q * turn
        for b in range(blocks):
            turned[u, pl.ds(b, azimuth, stride=blocks), :] = total[:, b * LANE : (b + 1) * LANE]
        send_all(turned, returned, send2, recv2, 1, u)

    for k in range(1, n_inst):
        mate(k).wait()
    instances = inst_dev * n_inst

    @pl.loop(0, variables)
    def _(v):
        @pl.loop(0, azimuth_dev)
        def _(t):
            for n in range(inst_dev):
                total = local[n, v, t]
                for k in range(n_inst):
                    for m in range(inst_dev):
                        offset = (n - m + k * inst_dev) % instances
                        value = state[m, v, t] if k == 0 else mates[k - 1, m, v, t]
                        total = total + (frequency[0] * time_row[offset]) * value
                local[n, v, t] = total

    for c in range(chunks):
        await_all(turned, returned, send2, recv2, 1, c)
        for i in range(inst_dev):
            for at_row in range(azimuth_dev * blocks):
                step, block = divmod(at_row, blocks)
                row = i * planes * span + at_row
                lanes = slice(block * LANE, (block + 1) * LANE)
                out[i, c, step, :, lanes] = (
                    local[i, c, step, :, lanes]
                    + returned[c, pl.ds(row, planes, stride=span), :]
                )
    for c in range(chunks):
        for route in [(0, 0)] + routes:
            exchange(outgoing, fields, send1, recv1, c, route).wait_send()
            exchange(turned, returned, send2, recv2, c, route).wait_send()


def on_device(
    flow_state,
    radial_first,
    radial_second,
    radial_flow,
    swirl_flow,
    radius_inverse,
    radial_flux,
    swirl_flux,
    cross_flux,
    span_flux,
    frequency,
    viscosity,
):
    inst_dev, variables, azimuth_dev, planes, radial = flow_state.shape
    n_inst = lax.axis_size("inst")
    n_space = lax.axis_size("space")
    azimuth = swirl_flow.shape[1]
    blocks = radial // LANE
    time_row = [float(x) for x in spectral_table(inst_dev * n_inst)[0][:, 0]]
    turn_first, turn_second = spectral_table(azimuth)
    h = np.float32(2.0 * math.pi / azimuth)
    turn = np.concatenate([h * turn_first, h * h * turn_second])
    turn_high = turn.astype(jnp.bfloat16)
    turn_low = (turn - turn_high.astype(np.float32)).astype(jnp.bfloat16)
    vmem = pl.BlockSpec(memory_space=pltpu.VMEM)
    hbm = pl.BlockSpec(memory_space=pltpu.HBM)
    smem = pl.BlockSpec(memory_space=pltpu.SMEM)
    packed = pltpu.VMEM((variables, azimuth * blocks, LANE), jnp.float32)
    slab = pltpu.VMEM((variables, azimuth, radial), jnp.float32)
    pencil = pltpu.VMEM((variables, azimuth_dev, planes, radial), jnp.float32)
    half_slab = pltpu.VMEM((azimuth, radial), jnp.bfloat16)
    square = pltpu.VMEM((radial, radial), jnp.bfloat16)
    sems = pltpu.SemaphoreType.DMA((variables, n_space))
    return pl.pallas_call(
        functools.partial(slab_kernel, n_space, n_inst, time_row),
        out_shape=pltpu.VMEM(flow_state.shape, jnp.float32),
        in_specs=[hbm] * 4 + [vmem] * 4 + [smem] * 6,
        out_specs=vmem,
        scratch_shapes=[
            pltpu.VMEM(flow_state.shape, jnp.float32),
            pltpu.VMEM((radial, radial), jnp.float32),
            pltpu.VMEM((radial, radial), jnp.float32),
            packed,
            packed,
            packed,
            packed,
            pltpu.VMEM((n_inst - 1,) + flow_state.shape, jnp.float32),
            pltpu.VMEM(flow_state.shape, jnp.float32),
            slab,
            slab,
            pencil,
            pencil,
            pltpu.VMEM((azimuth, radial), jnp.float32),
            square,
            square,
            square,
            square,
            half_slab,
            half_slab,
            sems,
            sems,
            sems,
            sems,
            pltpu.SemaphoreType.DMA((2, variables)),
            pltpu.SemaphoreType.DMA((n_inst - 1,)),
            pltpu.SemaphoreType.DMA((n_inst - 1,)),
            pltpu.SemaphoreType.DMA((variables + 3,)),
        ],
        compiler_params=pltpu.CompilerParams(
            collective_id=0, has_side_effects=True, vmem_limit_bytes=59 * 1024 * 1024
        ),
    )(
        flow_state,
        radial_first,
        radial_second,
        swirl_flow.T,
        radial_flow,
        radius_inverse.reshape(1, radial),
        jnp.asarray(turn_high),
        jnp.asarray(turn_low),
        radial_flux,
        swirl_flux,
        cross_flux,
        span_flux,
        frequency,
        viscosity,
    )


def residual_on_device(flow_state, *rest):
    inst_dev, variables, azimuth_dev, planes, radial = flow_state.shape
    blocks = radial // LANE
    slabs = (
        inst_dev * planes == lax.axis_size("space")
        and lax.axis_size("space") % 4 == 0
        and lax.axis_size("inst") > 1
        and planes == SUBLANE
        and radial == blocks * LANE
        and azimuth_dev * blocks % SUBLANE == 0
    )
    return (on_device if slabs else on_device_lines)(flow_state, *rest)


def solution(mesh):
    in_specs = (
        P("inst", None, "space", None, None),
        P(),
        P(),
        P("space", None),
        P(),
        P(),
        P(),
        P(),
        P(),
        P(),
        P(),
        P(),
    )
    out_specs = P("inst", None, "space", None, None)
    return jax.shard_map(
        residual_on_device, mesh=mesh, in_specs=in_specs, out_specs=out_specs, check_vma=False
    )
```
